32 devices in a mesh: ckpt: 4 (over x, core), wide: 8 (over z, y).
Axes of the slice: x: 2, y: 2, z: 4, core: 2. Of those that a mesh axis runs over, the one named last changes fastest.
Arguments:
- codes: bfloat16 [4, 8, 8192, 1024], P('ckpt', 'wide'), may hold values from -4 to 4
- scales: float32 [4, 8, 8192, 8], P('ckpt', 'wide'), may hold values from 0.5 to 5
- example_ids: int32 [8, 8192], P('wide'), may hold values from 0 to 8191, each once within a row
- targets: bfloat16 [1024, 4096], P('wide'), may hold values from -0.09375 to 0.09375
- owners: int32 [6], replicated, may hold values from 0 to 7, as said below
Outputs:
- scores: float32 [8, 8192, 768], P('wide', 'ckpt')
The draws below stay inside these ranges and needn't reach their ends.
Inputs may be any that keep to these rules, and one draw needn't show every extreme that they name: `example_ids`: each row is a permutation of the 8192 examples of its group. Distinct owners; owner 0 and owner 8 - 1 are always among them.
All inputs are finite; a program needn't handle non-finite values.
Results may differ from the reference program's by a relative error of at most 0.0029.
Values may be sent and summed in bfloat16 or wider, within the bound.
A program may use at most 192 MiB of HBM per device.

```python
import math
import jax
import jax.numpy as jnp
from jax import lax

K = 1024
C = 4
QB = 128
TBLK = 128
ROUNDS = 6
GROUPS = 8
GROUP_ROWS = 8192
TARGETS = 768
OWNED = 1024
CK = 4096
QBLOCKS = 8


def draw_owners(key, part):
    first_key = jax.random.fold_in(key, 17)
    second_key = jax.random.fold_in(key, 29)
    middle = 1 + jax.random.permutation(first_key, GROUPS - 2).astype(jnp.int32)
    picked = jnp.concatenate([middle[:ROUNDS - 2], jnp.array([0, GROUPS - 1], jnp.int32)])
    return jax.random.permutation(second_key, picked).astype(jnp.int32)


def shard_levels(stream_key, extent, pieces, low, high):
    factor_of = 1.0
    for dim, shards_of in pieces:
        draws = jax.random.uniform(jax.random.fold_in(jax.random.fold_in(stream_key, 6), dim), (shards_of,), jnp.float32, low / len(pieces), high / len(pieces))
        factor_of = factor_of * jnp.repeat(jnp.exp(draws), extent[dim] // shards_of).reshape((-1,) + (1,) * (len(extent) - 1 - dim))
    return factor_of


def noise(key, extent, spread, most, cuts=(), kind=jnp.bfloat16):
    factor_of = shard_levels(key, extent, cuts, -0.22, 0.18) if cuts else 1.0
    entries = jax.random.normal(key, extent, jnp.float32) * spread * factor_of
    return jnp.minimum(jnp.maximum(entries, -most), most).astype(kind)


def setup_inputs(seed: int = 0) -> dict:
    splits = jax.random.split(jax.random.key(seed), 6)
    return {
        "codes": noise(splits[0], (C, GROUPS, GROUP_ROWS, K), 1.0, 4.0, ((0, 4), (1, 8))),
        "scales": jnp.clip(jnp.exp(math.log(5.0) - 2.3025851 * jax.random.uniform(splits[1], (C, GROUPS, GROUP_ROWS, QBLOCKS), jnp.float32) ** shard_levels(splits[1], (C, GROUPS, GROUP_ROWS, QBLOCKS), ((0, 4), (1, 8)), -0.2, 0.2)), 0.5, 5.0),
        "example_ids": jax.vmap(lambda own: jax.random.permutation(own, GROUP_ROWS))(jax.random.split(splits[2], GROUPS)).reshape((GROUPS, GROUP_ROWS)).astype(jnp.int32),
        "targets": noise(splits[3], (OWNED, CK), CK ** -0.5, 0.09375, ((0, 8),)),
        "owners": draw_owners(jax.random.fold_in(splits[5], 71), 0),
    }


def reference(codes, scales, example_ids, targets, owners):
    blocks = targets.reshape(GROUPS, TBLK, CK)
    chosen = jnp.take(blocks, owners, axis=0).reshape(TARGETS, CK)

    def one_group(group):
        group_codes = lax.dynamic_index_in_dim(codes, group, 1, keepdims=False)
        group_scales = lax.dynamic_index_in_dim(scales, group, 1, keepdims=False)
        feats = (group_codes.astype(jnp.float32) * jnp.repeat(group_scales, QB, axis=-1)).astype(jnp.bfloat16)
        ids = lax.dynamic_index_in_dim(example_ids, group, 0, keepdims=False)
        picked = jnp.take(feats, ids, axis=1)
        resident = jnp.transpose(picked, (1, 0, 2)).reshape(GROUP_ROWS, CK)
        total = lax.dot_general(resident, chosen, (((1,), (1,)), ((), ())), preferred_element_type=jnp.float32)
        return total * (1.0 / C)

    return lax.map(one_group, jnp.arange(GROUPS, dtype=jnp.int32))
```

```python
import jax
import jax.numpy as jnp
from jax import lax
from jax.sharding import PartitionSpec as P

PIECES = 4


def swap(value, distance, size):
    return lax.ppermute(value, "ckpt", [(i, i ^ distance) for i in range(size)])


def per_device(codes, scales, example_ids, targets, owners):
    me = lax.axis_index("ckpt")
    size = lax.axis_size("ckpt")
    width = codes.shape[-1]
    blocks = scales.shape[-1]
    block = width // blocks
    per_owner = targets.shape[0]
    rounds = owners.shape[0]
    rows = codes.shape[2]
    own_rows = rows // size
    piece_rows = own_rows // PIECES

    piece = lax.dynamic_slice_in_dim(targets, me * width, width, 1)
    everyone = lax.all_gather(piece, "wide", axis=0)
    chosen = jnp.take(everyone, owners, axis=0).reshape(rounds * per_owner, width)

    feats = (codes[0, 0].astype(jnp.float32) * jnp.repeat(scales[0, 0], block, axis=-1)).astype(
        jnp.bfloat16
    )
    ordered = jnp.take(feats, example_ids[0], axis=0, mode="clip", unique_indices=True)
    ordered = ordered.reshape(size, PIECES, piece_rows, width)
    contract = (((1,), (1,)), ((), ()))

    def partial(home, step):
        part = lax.dynamic_index_in_dim(ordered[:, step], home, 0, keepdims=False)
        return lax.dot_general(part, chosen, contract, preferred_element_type=jnp.float32)

    factor = 1.0 / size
    pieces = []
    for step in range(PIECES):
        far_pair = partial(me ^ 3, step).astype(jnp.bfloat16)
        near_pair = partial(me ^ 1, step).astype(jnp.bfloat16)
        far = partial(me ^ 2, step) + swap(far_pair, 1, size).astype(jnp.float32)
        near = partial(me, step) + swap(near_pair, 1, size).astype(jnp.float32)
        total = near + swap(far.astype(jnp.bfloat16), 2, size).astype(jnp.float32)
        pieces.append(total * factor)
    return jnp.concatenate(pieces, axis=0)[None]


def solution(mesh):
    return jax.shard_map(
        per_device,
        mesh=mesh,
        in_specs=(
            P("ckpt", "wide", None, None),
            P("ckpt", "wide", None, None),
            P("wide", None),
            P("wide", None),
            P(),
        ),
        out_specs=P("wide", "ckpt", None),
        check_vma=False,
    )
```

```python
import functools

import jax
import jax.numpy as jnp
from jax import lax
from jax.experimental import pallas as pl
from jax.experimental.pallas import tpu as pltpu
from jax.sharding import PartitionSpec as P

PIECES = 4
TILE_ROWS = 512
UNROLL = 32


def order_kernel(tiles, ids_ref, codes_ref, scales_ref, out_ref, feats, picked):
    step = pl.program_id(0)
    tile_rows, width = codes_ref.shape
    blocks = scales_ref.shape[1]
    block = width // blocks

    @pl.when(step < tiles)
    def scale():
        first = step * (tile_rows * blocks)
        for q in range(blocks):
            codes = codes_ref[:, q * block : (q + 1) * block].astype(jnp.float32)
            value = (codes * scales_ref[:, q : q + 1]).astype(jnp.bfloat16)
            feats[pl.ds(first + q, tile_rows, stride=blocks), :] = value.astype(jnp.float32)

    @pl.when(step >= tiles)
    def order():
        base = (step - tiles) * tile_rows

        def some(i, carry):
            at = i * UNROLL
            rows = [
                feats[pl.ds(pl.multiple_of(ids_ref[base + at + u] * blocks, blocks), blocks), :]
                for u in range(UNROLL)
            ]
            for u in range(UNROLL):
                to = pl.multiple_of((at + u) * blocks, blocks)
                picked[pl.ds(to, blocks), :] = rows[u]
            return carry

        lax.fori_loop(0, tile_rows // UNROLL, some, 0)
        for q in range(blocks):
            out_ref[:, q * block : (q + 1) * block] = picked[
                pl.ds(q, tile_rows, stride=blocks), :
            ].astype(out_ref.dtype)


def order_rows(codes, scales, ids):
    rows, width = codes.shape
    blocks = scales.shape[1]
    block = width // blocks
    tiles = rows // TILE_ROWS
    return pl.pallas_call(
        functools.partial(order_kernel, tiles),
        grid=(2 * tiles,),
        in_specs=[
            pl.BlockSpec(memory_space=pltpu.SMEM),
            pl.BlockSpec((TILE_ROWS, width), lambda s: (jnp.minimum(s, tiles - 1), 0)),
            pl.BlockSpec((TILE_ROWS, blocks), lambda s: (jnp.minimum(s, tiles - 1), 0)),
        ],
        out_specs=pl.BlockSpec((TILE_ROWS, width), lambda s: (jnp.maximum(s - tiles, 0), 0)),
        out_shape=jax.ShapeDtypeStruct((rows, width), jnp.bfloat16),
        scratch_shapes=[
            pltpu.VMEM((rows * blocks, block), jnp.float32),
            pltpu.VMEM((TILE_ROWS * blocks, block), jnp.float32),
        ],
        compiler_params=pltpu.CompilerParams(vmem_limit_bytes=50 * 2**20),
        cost_estimate=pl.CostEstimate(
            flops=rows * width * 100, bytes_accessed=rows * width * 8, transcendentals=0
        ),
    )(ids, codes, scales)


def swap(value, distance, size):
    return lax.ppermute(value, "ckpt", [(i, i ^ distance) for i in range(size)])


def per_device(codes, scales, example_ids, targets, owners):
    me = lax.axis_index("ckpt")
    size = lax.axis_size("ckpt")
    width = codes.shape[-1]
    per_owner = targets.shape[0]
    rounds = owners.shape[0]
    rows = codes.shape[2]
    own_rows = rows // size
    piece_rows = own_rows // PIECES

    piece = lax.dynamic_slice_in_dim(targets, me * width, width, 1)
    everyone = lax.all_gather(piece, "wide", axis=0)
    chosen = jnp.take(everyone, owners, axis=0).reshape(rounds * per_owner, width)

    ordered = order_rows(codes[0, 0], scales[0, 0], example_ids[0])
    contract = (((1,), (1,)), ((), ()))

    def partial(home, step):
        part = lax.dynamic_slice_in_dim(ordered, home * own_rows + step * piece_rows, piece_rows, 0)
        return lax.dot_general(part, chosen, contract, preferred_element_type=jnp.float32)

    factor = 1.0 / size
    pieces = []
    for step in range(PIECES):
        far_pair = partial(me ^ 3, step).astype(jnp.bfloat16)
        near_pair = partial(me ^ 1, step).astype(jnp.bfloat16)
        far = partial(me ^ 2, step) + swap(far_pair, 1, size).astype(jnp.float32)
        near = partial(me, step) + swap(near_pair, 1, size).astype(jnp.float32)
        total = near + swap(far.astype(jnp.bfloat16), 2, size).astype(jnp.float32)
        pieces.append(total * factor)
    return jnp.concatenate(pieces, axis=0)[None]


def solution(mesh):
    return jax.shard_map(
        per_device,
        mesh=mesh,
        in_specs=(
            P("ckpt", "wide", None, None),
            P("ckpt", "wide", None, None),
            P("wide", None),
            P("wide", None),
            P(),
        ),
        out_specs=P("wide", "ckpt", None),
        check_vma=False,
    )
```

```python
import functools

import jax
import jax.numpy as jnp
from jax import lax
from jax.experimental import pallas as pl
from jax.experimental.pallas import tpu as pltpu
from jax.sharding import PartitionSpec as P

TILE_ROWS = 512
UNROLL = 32


def order_kernel(tiles, ids_ref, codes_ref, scales_ref, out_ref, feats, picked):
    step = pl.program_id(0)
    tile_rows, width = codes_ref.shape
    blocks = scales_ref.shape[1]
    block = width // blocks

    @pl.when(step < tiles)
    def scale():
        first = step * (tile_rows * blocks)
        for q in range(blocks):
            codes = codes_ref[:, q * block : (q + 1) * block].astype(jnp.float32)
            value = (codes * scales_ref[:, q : q + 1]).astype(jnp.bfloat16)
            feats[pl.ds(first + q, tile_rows, stride=blocks), :] = value.astype(jnp.float32)

    @pl.when(step >= tiles)
    def order():
        base = (step - tiles) * tile_rows

        def some(i, carry):
            at = i * UNROLL
            rows = [
                feats[pl.ds(pl.multiple_of(ids_ref[base + at + u] * blocks, blocks), blocks), :]
                for u in range(UNROLL)
            ]
            for u in range(UNROLL):
                to = pl.multiple_of((at + u) * blocks, blocks)
                picked[pl.ds(to, blocks), :] = rows[u]
            return carry

        lax.fori_loop(0, tile_rows // UNROLL, some, 0)
        for q in range(blocks):
            out_ref[:, q * block : (q + 1) * block] = picked[
                pl.ds(q, tile_rows, stride=blocks), :
            ].astype(out_ref.dtype)


def order_rows(codes, scales, ids):
    rows, width = codes.shape
    blocks = scales.shape[1]
    block = width // blocks
    tiles = rows // TILE_ROWS
    return pl.pallas_call(
        functools.partial(order_kernel, tiles),
        grid=(2 * tiles,),
        in_specs=[
            pl.BlockSpec(memory_space=pltpu.SMEM),
            pl.BlockSpec((TILE_ROWS, width), lambda s: (jnp.minimum(s, tiles - 1), 0)),
            pl.BlockSpec((TILE_ROWS, blocks), lambda s: (jnp.minimum(s, tiles - 1), 0)),
        ],
        out_specs=pl.BlockSpec((TILE_ROWS, width), lambda s: (jnp.maximum(s - tiles, 0), 0)),
        out_shape=jax.ShapeDtypeStruct((rows, width), jnp.bfloat16),
        scratch_shapes=[
            pltpu.VMEM((rows * blocks, block), jnp.float32),
            pltpu.VMEM((TILE_ROWS * blocks, block), jnp.float32),
        ],
        compiler_params=pltpu.CompilerParams(vmem_limit_bytes=50 * 2**20),
        cost_estimate=pl.CostEstimate(
            flops=rows * width * 100, bytes_accessed=rows * width * 8, transcendentals=0
        ),
    )(ids, codes, scales)


def swap(value, distance, size):
    return lax.ppermute(value, "ckpt", [(i, i ^ distance) for i in range(size)])


def per_device(codes, scales, example_ids, targets, owners):
    me = lax.axis_index("ckpt")
    size = lax.axis_size("ckpt")
    width = codes.shape[-1]
    per_owner = targets.shape[0]
    rounds = owners.shape[0]
    rows = codes.shape[2]
    own_rows = rows // size

    piece = lax.dynamic_slice_in_dim(targets, me * width, width, 1)
    everyone = lax.all_gather(piece, "wide", axis=0)
    chosen = jnp.take(everyone, owners, axis=0, mode="clip").reshape(rounds * per_owner, width)

    ordered = order_rows(codes[0, 0], scales[0, 0], example_ids[0])
    contract = (((1,), (1,)), ((), ()))

    def partial(home, start, extent):
        part = lax.dynamic_slice_in_dim(ordered, home * own_rows + start, extent, 0)
        return lax.dot_general(part, chosen, contract, preferred_element_type=jnp.float32)

    factor = 1.0 / size
    eighth = own_rows // 8
    cuts = [0, 1, 3, 5, 7, 8]
    spans = [(lo * eighth, (hi - lo) * eighth) for lo, hi in zip(cuts, cuts[1:])]
    crossed = []
    for start, extent in spans:
        far_pair = partial(me ^ 3, start, extent).astype(jnp.bfloat16)
        far = partial(me ^ 2, start, extent) + swap(far_pair, 1, size).astype(jnp.float32)
        far = far.astype(jnp.bfloat16)
        crossed.append(swap(far, 2, size))
    chosen, crossed[0] = lax.optimization_barrier((chosen, crossed[0]))
    pieces = []
    for (start, extent), other in zip(spans, crossed):
        near_pair = partial(me ^ 1, start, extent).astype(jnp.bfloat16)
        near = partial(me, start, extent) + swap(near_pair, 1, size).astype(jnp.float32)
        pieces.append((near + other.astype(jnp.float32)) * factor)
    return jnp.concatenate(pieces, axis=0)[None]


def solution(mesh):
    return jax.shard_map(
        per_device,
        mesh=mesh,
        in_specs=(
            P("ckpt", "wide", None, None),
            P("ckpt", "wide", None, None),
            P("wide", None),
            P("wide", None),
            P(),
        ),
        out_specs=P("wide", "ckpt", None),
        check_vma=False,
    )
```

```python
import functools

import jax
import jax.numpy as jnp
from jax import lax
from jax.experimental import pallas as pl
from jax.experimental.pallas import tpu as pltpu
from jax.sharding import PartitionSpec as P

TILE_ROWS = 512
UNROLL = 32


def order_kernel(tiles, ids_ref, codes_ref, scales_ref, out_ref, feats, picked):
    step = pl.program_id(0)
    tile_rows, width = codes_ref.shape
    blocks = scales_ref.shape[1]
    block = width // blocks

    @pl.when(step < tiles)
    def scale():
        first = step * (tile_rows * blocks)
        for q in range(blocks):
            codes = codes_ref[:, q * block : (q + 1) * block].astype(jnp.float32)
            value = (codes * scales_ref[:, q : q + 1]).astype(jnp.bfloat16)
            feats[pl.ds(first + q, tile_rows, stride=blocks), :] = value.astype(jnp.float32)

    @pl.when(step >= tiles)
    def order():
        base = (step - tiles) * tile_rows

        def some(i, carry):
            at = i * UNROLL
            rows = [
                feats[pl.ds(pl.multiple_of(ids_ref[base + at + u] * blocks, blocks), blocks), :]
                for u in range(UNROLL)
            ]
            for u in range(UNROLL):
                to = pl.multiple_of((at + u) * blocks, blocks)
                picked[pl.ds(to, blocks), :] = rows[u]
            return carry

        lax.fori_loop(0, tile_rows // UNROLL, some, 0)
        for q in range(blocks):
            out_ref[:, q * block : (q + 1) * block] = picked[
                pl.ds(q, tile_rows, stride=blocks), :
            ].astype(out_ref.dtype)


def order_rows(codes, scales, ids):
    rows, width = codes.shape
    blocks = scales.shape[1]
    block = width // blocks
    tiles = rows // TILE_ROWS
    return pl.pallas_call(
        functools.partial(order_kernel, tiles),
        grid=(2 * tiles,),
        in_specs=[
            pl.BlockSpec(memory_space=pltpu.SMEM),
            pl.BlockSpec((TILE_ROWS, width), lambda s: (jnp.minimum(s, tiles - 1), 0)),
            pl.BlockSpec((TILE_ROWS, blocks), lambda s: (jnp.minimum(s, tiles - 1), 0)),
        ],
        out_specs=pl.BlockSpec((TILE_ROWS, width), lambda s: (jnp.maximum(s - tiles, 0), 0)),
        out_shape=jax.ShapeDtypeStruct((rows, width), jnp.bfloat16),
        scratch_shapes=[
            pltpu.VMEM((rows * blocks, block), jnp.float32),
            pltpu.VMEM((TILE_ROWS * blocks, block), jnp.float32),
        ],
        compiler_params=pltpu.CompilerParams(vmem_limit_bytes=50 * 2**20),
        cost_estimate=pl.CostEstimate(
            flops=rows * width * 100, bytes_accessed=rows * width * 8, transcendentals=0
        ),
    )(ids, codes, scales)


def swap(value, distance, size):
    return lax.ppermute(value, "ckpt", [(i, i ^ distance) for i in range(size)])


def per_device(codes, scales, example_ids, targets, owners):
    me = lax.axis_index("ckpt")
    size = lax.axis_size("ckpt")
    width = codes.shape[-1]
    per_owner = targets.shape[0]
    rounds = owners.shape[0]
    rows = codes.shape[2]
    own_rows = rows // size

    piece = lax.dynamic_slice_in_dim(targets, me * width, width, 1)
    half = per_owner // 2
    gathered = [lax.all_gather(p, "wide", axis=0) for p in (piece[:half], piece[half:])]

    ordered = order_rows(codes[0, 0], scales[0, 0], example_ids[0])
    contract = (((1,), (1,)), ((), ()))

    def partial(home, start, extent, chosen):
        part = lax.dynamic_slice_in_dim(ordered, home * own_rows + start, extent, 0)
        return lax.dot_general(part, chosen, contract, preferred_element_type=jnp.float32)

    factor = 1.0 / size
    eighth = own_rows // 8
    cuts = [0, 2, 4, 6, 8]
    spans = [(lo * eighth, (hi - lo) * eighth) for lo, hi in zip(cuts, cuts[1:])]

    def choose(everyone):
        return jnp.take(everyone, owners, axis=0, mode="clip")

    def summed(start, extent, columns):
        far_pair = partial(me ^ 3, start, extent, columns).astype(jnp.bfloat16)
        far = partial(me ^ 2, start, extent, columns)
        return (far + swap(far_pair, 1, size).astype(jnp.float32)).astype(jnp.bfloat16)

    early = choose(gathered[0])
    sent = summed(*spans[0], early.reshape(rounds * half, width))
    split = [swap(sent, 2, size)]
    late, split[0] = lax.optimization_barrier((gathered[1], split[0]))
    late = choose(late)
    sent = summed(*spans[0], late.reshape(rounds * half, width))
    split.append(swap(sent, 2, size))
    late, _ = lax.optimization_barrier((late, sent))
    chosen = jnp.concatenate([early, late], axis=1).reshape(rounds * per_owner, width)
    crossed = [swap(summed(*span, chosen), 2, size) for span in spans[1:]]
    split = [part.reshape(-1, rounds, half) for part in split]
    split[0], split[1], chosen = lax.optimization_barrier((split[0], split[1], chosen))
    first = jnp.concatenate(split, axis=2).reshape(-1, rounds * per_owner)
    crossed.insert(0, first)
    pieces = []
    for (start, extent), other in zip(spans, crossed):
        near_pair = partial(me ^ 1, start, extent, chosen).astype(jnp.bfloat16)
        near = partial(me, start, extent, chosen)
        near = near + swap(near_pair, 1, size).astype(jnp.float32)
        pieces.append((near + other.astype(jnp.float32)) * factor)
    return jnp.concatenate(pieces, axis=0)[None]


def solution(mesh):
    return jax.shard_map(
        per_device,
        mesh=mesh,
        in_specs=(
            P("ckpt", "wide", None, None),
            P("ckpt", "wide", None, None),
            P("wide", None),
            P("wide", None),
            P(),
        ),
        out_specs=P("wide", "ckpt", None),
        check_vma=False,
    )
```
